256 devices in a mesh: row: 16 (over z, y_hi), col: 16 (over x, y_lo, core).
Axes of the slice: x: 4, y: 4 (y_hi: 2, y_lo: 2; y = y_hi * 2 + y_lo), z: 8, core: 2. Of those that a mesh axis runs over, the one named last changes fastest.
Arguments:
- hidden: bfloat16 [1024, 28672], P('col', 'row'), may hold values from -6 to 6
- down_weight: bfloat16 [28672, 8192], P('row', 'col'), may hold values from -0.03125 to 0.03125
- out_grad: bfloat16 [1024, 8192], P('row', 'col'), may hold values from -6 to 6
Outputs:
- projected: bfloat16 [1024, 8192], P('row', 'col')
- hidden_grad: bfloat16 [1024, 28672], P('col', 'row')
- weight_grad: float32 [28672, 8192], P('row', 'col')
The draws below stay inside these ranges and needn't reach their ends.
All inputs are finite; a program needn't handle non-finite values.
Results may differ from the reference program's by a relative error of at most 0.001.
Values may be sent and summed in bfloat16 or wider, within the bound.
No kernel may reach another device: no remote copies, remote signals or barrier semaphores. Data moves between devices by JAX's collectives and lax.ppermute only.
A program may use at most 64 MiB of HBM per device.

```python
import jax
import jax.numpy as jnp
from jax import lax

D = 8192
FF = 28672
TOKENS = 1024


def raised(drawn, own_key, source, target, blocks, factor):
    def block_of(axis_at):
        return (jnp.arange(drawn.shape[axis_at]) // (drawn.shape[axis_at] // blocks)).reshape((-1,) + (1,) * (drawn.ndim - 1 - axis_at))

    near = jax.random.permutation(own_key, blocks)[block_of(target)]
    other_side = (block_of(target) + blocks // 2) % blocks
    return jnp.where((block_of(source) == near) | (block_of(source) == other_side), factor * drawn, drawn)


def levels(key, extent, pieces, least, high):
    loudness, own = 1.0, jax.random.fold_in(key, 6)
    for dim, shards_of in pieces:
        draws = jnp.exp(jax.random.uniform(jax.random.fold_in(own, dim), (shards_of,), jnp.float32, least / len(pieces), high / len(pieces)))
        loudness = loudness * jnp.repeat(draws, extent[dim] // shards_of).reshape([-1 if axis == dim else 1 for axis in range(len(extent))])
    return loudness


def noise(stream_key, dims, width, reach, pieces=(), kind=jnp.bfloat16):
    gain = levels(stream_key, dims, pieces, -0.22, 0.18) if pieces else 1.0
    values = jax.random.normal(stream_key, dims, jnp.float32) * width * gain
    return jnp.minimum(jnp.maximum(values, -reach), reach).astype(kind)


def noise_with(rng, shape, width, reach, pieces, heavy, dtype=jnp.bfloat16):
    values = width * jax.random.normal(rng, shape, jnp.float32)
    if pieces:
        values = values * levels(rng, shape, pieces, -0.22, 0.18)
    return jnp.clip(raised(values, jax.random.fold_in(rng, 3), *heavy), -reach, reach).astype(dtype)


def setup_inputs(seed: int = 0) -> dict:
    key_list = jax.random.split(jax.random.key(seed), 4)
    return {
        "hidden": noise_with(key_list[0], (TOKENS, FF), 1.0, 6.0, ((0, 16), (1, 16)), (1, 0, 16, 2.0)),
        "down_weight": noise(key_list[1], (FF, D), FF ** -0.5, 0.03125, ((0, 16), (1, 16))),
        "out_grad": noise_with(key_list[2], (TOKENS, D), 1.0, 6.0, ((0, 16), (1, 16)), (1, 0, 16, 2.0)),
    }


def reference(hidden, down_weight, out_grad):
    projected = jnp.dot(hidden, down_weight, preferred_element_type=jnp.float32).astype(jnp.bfloat16)
    hidden_grad = lax.dot_general(out_grad, down_weight, (((1,), (1,)), ((), ())), preferred_element_type=jnp.float32).astype(jnp.bfloat16)
    weight_grad = lax.dot_general(hidden, out_grad, (((0,), (0,)), ((), ())), preferred_element_type=jnp.float32)
    weight_grad = weight_grad / jnp.sqrt(jnp.float32(TOKENS))
    return (projected, hidden_grad, weight_grad)
```

```python
import jax
import jax.numpy as jnp
from jax import lax
from jax.experimental import pallas as pl
from jax.experimental.pallas import tpu as pltpu
from jax.sharding import PartitionSpec as P


BF = jnp.bfloat16
F32 = jnp.float32
SPAN = 248.0


def encode(out, x):
    n = x.shape[1]
    top = jnp.max(jnp.abs(x), axis=1, keepdims=True) * (1 + 2.0**-7)
    top = jnp.maximum(top, 1e-36).astype(BF).astype(F32)
    code = jnp.exp2(jnp.abs(x) * (SPAN / top) - SPAN / 2)
    out[:, :n] = jnp.where(x < 0, -code, code).astype(BF)
    out[:, n:] = jnp.broadcast_to(top, (x.shape[0], 128)).astype(BF)


def decode(ref, n):
    code = ref[:, :n].astype(F32)
    top = ref[:, n : n + 1].astype(F32)
    size = (jnp.log2(jnp.abs(code)) + SPAN / 2) * (top * (1 / SPAN))
    return jnp.where(code < 0, -size, size)


def position():
    row, col = lax.axis_index("row"), lax.axis_index("col")
    return row // 2, row % 2, col // 2, col % 2


def grad_kernel(*refs):
    z, _, chip, _ = position()
    rings, (w_own, w_other), outs = refs[:8], refs[8:10], refs[10:20]
    ring, lhs, acc = refs[20:]
    own, sends, g_own, g_other = outs[0], outs[1:8], outs[8], outs[9]
    width = w_own.shape[1]
    for s in range(8):
        ring[s] = rings[s][...]
    for k in range(8):
        rows = pl.ds(k * 64, 64)
        for half, keep in enumerate((g_own, g_other)):
            block = ring[(jnp.bitwise_xor(chip, k) - z + 8) % 8, half]
            lhs[rows, half * width : (half + 1) * width] = block
            keep[rows, :] = block
    dims = (((1,), (1,)), ((), ()))
    for n in range(w_own.shape[0] // 256):
        cols = pl.ds(n * 256, 256)
        acc[:, n * 256 : (n + 1) * 256] = lax.dot_general(
            lhs[:, :width], w_own[cols, :], dims, preferred_element_type=F32
        ) + lax.dot_general(lhs[:, width:], w_other[cols, :], dims, preferred_element_type=F32)
    own[...] = acc[:64]
    for k in range(1, 8):
        encode(sends[k - 1], acc[k * 64 : (k + 1) * 64])


def proj_kernel(*refs):
    z, _, chip, _ = position()
    blocks, (w_own, w_other), outs = refs[:8], refs[8:10], refs[10:19]
    lhs, acc = refs[19:]
    own, sends, h_all = outs[0], outs[1:8], outs[8]
    width = w_own.shape[1]
    for k in range(8):
        lhs[k * 64 : (k + 1) * 64] = blocks[k][...]
    h_all[...] = lhs[...]
    for half, w in enumerate((w_own, w_other)):
        for n in range(width // 256):
            at = half * width + n * 256
            res = jnp.dot(lhs[...], w[:, n * 256 : (n + 1) * 256], preferred_element_type=F32)
            acc[:, :, at : at + 256] = res.reshape(8, 64, 256)
    own[...] = acc[jnp.bitwise_xor(chip, z)]
    for s in range(1, 8):
        encode(sends[s - 1], acc[jnp.bitwise_xor(chip, (z + s) % 8)])


def sum_hidden_kernel(*refs):
    own, codes, out = refs[0], refs[1:8], refs[8]
    total = own[...]
    for code in codes:
        total = total + decode(code, own.shape[1])
    out[...] = total.astype(BF)


def sum_proj_kernel(*refs):
    own, codes, out_own, out_other, out_first = refs[0], refs[1:8], *refs[8:]
    _, y, _, core = position()
    total = own[...]
    for code in codes:
        total = total + decode(code, own.shape[1])
    width = own.shape[1] // 2
    out_own[...] = total[:, :width]
    out_other[...] = total[:, width:]
    out_first[...] = jnp.where(y == core, total[:, width:], total[:, :width])


def call(kernel, out_shape, scratch, *args):
    vmem = pl.BlockSpec(memory_space=pltpu.VMEM)
    return pl.pallas_call(
        kernel,
        out_shape=out_shape,
        in_specs=[vmem] * len(args),
        out_specs=[vmem] * len(out_shape),
        scratch_shapes=scratch,
        compiler_params=pltpu.CompilerParams(vmem_limit_bytes=24 * 2**20),
    )(*map(near, args))


def near(x):
    return pltpu.with_memory_space_constraint(x, pltpu.VMEM)


def col_send(x, k):
    return lax.ppermute(x, "col", [(i, i ^ k) for i in range(16)])


def z_send(x, s):
    return lax.ppermute(x, "row", [(i, (i + 2 * s) % 16) for i in range(16)])


def on_chip_row(source_of, keep=lambda y, core: True):
    pairs = []
    for row in range(16):
        for col in range(16):
            y, core = row % 2, col % 2
            if keep(y, core):
                from_y, from_core = source_of(y, core)
                pairs.append(((row - y + from_y) * 16 + col - core + from_core, row * 16 + col))
    return pairs


def on_device(hidden, weight, out_grad):
    hidden, weight = near(hidden), near(weight)
    tokens, units = hidden.shape
    width = weight.shape[1]
    both = ("row", "col")
    _, y, _, core = position()
    same = y == core
    opposite = on_chip_row(lambda y, core: (1 - y, 1 - core), lambda y, core: y != core)

    beside = on_chip_row(lambda y, core: (y, 1 - core) if y == core else (1 - y, core))
    first = lax.ppermute(out_grad, both, beside)
    second = lax.ppermute(out_grad, both, opposite)
    ring = [None] * 8
    ring[0] = jnp.stack([jnp.where(same, out_grad, first), jnp.where(same, first, second)])
    for s in range(1, 4):
        ring[s] = z_send(ring[s - 1], -1)
        ring[8 - s] = z_send(ring[(9 - s) % 8], 1)
    ring[4] = z_send(ring[3], -1)
    other_weight = col_send(weight, 1)

    blocks = [None] * 8
    blocks[0] = hidden
    blocks[1] = col_send(hidden, 2)
    for k in (2, 6, 4):
        blocks[k] = col_send(hidden, 2 * k)
        blocks[k + 1] = col_send(blocks[1], 2 * k)

    half = 8 * tokens
    shape = jax.ShapeDtypeStruct
    grad_out = call(
        grad_kernel,
        [shape((tokens, units), F32)]
        + [shape((tokens, units + 128), BF)] * 7
        + [shape((half, width), BF)] * 2,
        [
            pltpu.VMEM((8, 2, tokens, width), BF),
            pltpu.VMEM((half, 2 * width), BF),
            pltpu.VMEM((half, units), F32),
        ],
        *ring,
        weight,
        other_weight,
    )
    proj_out = call(
        proj_kernel,
        [shape((tokens, 2 * width), F32)]
        + [shape((tokens, 2 * width + 128), BF)] * 7
        + [shape((half, units), BF)],
        [
            pltpu.VMEM((half, units), BF),
            pltpu.VMEM((8, tokens, 2 * width), F32),
        ],
        *blocks,
        weight,
        other_weight,
    )
    got_grad = [col_send(grad_out[k], 2 * k) for k in (4, 6, 2, 5, 7, 3, 1)]
    got_proj = [z_send(proj_out[s], s) for s in (4, 3, 5, 2, 6, 1, 7)]
    g_own, g_swap = grad_out[8], col_send(grad_out[9], 1)
    h_own, h_swap = proj_out[8], col_send(proj_out[8], 1)

    dims = (((0,), (0,)), ((), ()))
    weight_grad = lax.dot_general(h_own, g_own, dims, preferred_element_type=F32)
    weight_grad += lax.dot_general(h_swap, g_swap, dims, preferred_element_type=F32)
    weight_grad = weight_grad / jnp.sqrt(F32(16 * tokens))

    (hidden_grad,) = call(
        sum_hidden_kernel, [shape((tokens, units), BF)], [], grad_out[0], *got_grad
    )
    sum_own, sum_other, sum_first = call(
        sum_proj_kernel, [shape((tokens, width), F32)] * 3, [], proj_out[0], *got_proj
    )
    beside = on_chip_row(lambda y, core: (1 - y, core) if y == core else (y, 1 - core))
    first = lax.ppermute(sum_first, both, beside)
    second = lax.ppermute(sum_other, both, opposite)
    projected = (first + jnp.where(same, sum_own, second)).astype(BF)
    return (projected, hidden_grad, weight_grad)


def solution(mesh):
    return jax.shard_map(
        on_device,
        mesh=mesh,
        in_specs=(P("col", "row"), P("row", "col"), P("row", "col")),
        out_specs=(P("row", "col"), P("col", "row"), P("row", "col")),
        check_vma=False,
    )
```

```python
import jax
import jax.numpy as jnp
from jax import lax
from jax.experimental import pallas as pl
from jax.experimental.pallas import tpu as pltpu
from jax.sharding import PartitionSpec as P


BF = jnp.bfloat16
F32 = jnp.float32
SPAN = 248.0


def encode(out, x):
    n = x.shape[1]
    top = jnp.max(jnp.abs(x), axis=1, keepdims=True) * (1 + 2.0**-7)
    top = jnp.maximum(top, 1e-36).astype(BF).astype(F32)
    code = jnp.exp2(jnp.abs(x) * (SPAN / top) - SPAN / 2)
    out[:, :n] = jnp.where(x < 0, -code, code).astype(BF)
    out[:, n:] = jnp.broadcast_to(top, (x.shape[0], 128)).astype(BF)


def decode(ref, n):
    code = ref[:, :n].astype(F32)
    top = ref[:, n : n + 1].astype(F32)
    size = (jnp.log2(jnp.abs(code)) + SPAN / 2) * (top * (1 / SPAN))
    return jnp.where(code < 0, -size, size)


def position():
    row, col = lax.axis_index("row"), lax.axis_index("col")
    return row // 2, row % 2, col // 2, col % 2


def grad_kernel(*refs):
    z, _, chip, _ = position()
    rings, (w_own, w_other), outs = refs[:8], refs[8:10], refs[10:20]
    ring, lhs, acc = refs[20:]
    own, sends, g_own, g_other = outs[0], outs[1:8], outs[8], outs[9]
    width = w_own.shape[1]
    for s in range(8):
        ring[s] = rings[s][...]
    for k in range(8):
        rows = pl.ds(k * 64, 64)
        for half, keep in enumerate((g_own, g_other)):
            block = ring[(jnp.bitwise_xor(chip, k) - z + 8) % 8, half]
            lhs[rows, half * width : (half + 1) * width] = block
            keep[rows, :] = block
    dims = (((1,), (1,)), ((), ()))
    for n in range(w_own.shape[0] // 256):
        cols = pl.ds(n * 256, 256)
        acc[:, n * 256 : (n + 1) * 256] = lax.dot_general(
            lhs[:, :width], w_own[cols, :], dims, preferred_element_type=F32
        ) + lax.dot_general(lhs[:, width:], w_other[cols, :], dims, preferred_element_type=F32)
    own[...] = acc[:64]
    for k in range(1, 8):
        encode(sends[k - 1], acc[k * 64 : (k + 1) * 64])


def proj_kernel(*refs):
    z, _, chip, _ = position()
    blocks, (w_own, w_other), outs = refs[:8], refs[8:10], refs[10:19]
    lhs, acc = refs[19:]
    own, sends, h_all = outs[0], outs[1:8], outs[8]
    width = w_own.shape[1]
    for k in range(8):
        lhs[k * 64 : (k + 1) * 64] = blocks[k][...]
    h_all[...] = lhs[...]
    for half, w in enumerate((w_own, w_other)):
        for n in range(width // 256):
            at = half * width + n * 256
            res = jnp.dot(lhs[...], w[:, n * 256 : (n + 1) * 256], preferred_element_type=F32)
            acc[:, :, at : at + 256] = res.reshape(8, 64, 256)
    own[...] = acc[jnp.bitwise_xor(chip, z)]
    for s in range(1, 8):
        encode(sends[s - 1], acc[jnp.bitwise_xor(chip, (z + s) % 8)])


def load_kernel(*refs):
    sems = refs[-1]
    copies = [pltpu.make_async_copy(refs[i], refs[2 + i], sems.at[i]) for i in range(2)]
    for copy in copies:
        copy.start()
    for copy in copies:
        copy.wait()


def sum_hidden_kernel(own, *refs):
    codes, out = refs[:-1], refs[-1]
    total = own[...]
    for code in codes:
        total = total + decode(code, own.shape[1])
    out[...] = total.astype(out.dtype)


def sum_proj_kernel(*refs):
    own, codes, out_own, out_other, out_first = refs[0], refs[1:8], *refs[8:]
    _, y, _, core = position()
    total = own[...]
    for code in codes:
        total = total + decode(code, own.shape[1])
    width = own.shape[1] // 2
    out_own[...] = total[:, :width]
    out_other[...] = total[:, width:]
    out_first[...] = jnp.where(y == core, total[:, width:], total[:, :width])


def call(kernel, out_shape, scratch, *args, place=None):
    vmem = pl.BlockSpec(memory_space=pltpu.VMEM)
    place = place or near
    return pl.pallas_call(
        kernel,
        out_shape=out_shape,
        in_specs=[vmem if place is near else pl.BlockSpec(memory_space=pltpu.HBM)] * len(args),
        out_specs=[vmem] * len(out_shape),
        scratch_shapes=scratch,
        compiler_params=pltpu.CompilerParams(vmem_limit_bytes=24 * 2**20),
    )(*map(place, args))


def far(x):
    return pltpu.with_memory_space_constraint(x, pltpu.HBM)


def near(x):
    return pltpu.with_memory_space_constraint(x, pltpu.VMEM)


def col_send(x, k):
    return lax.ppermute(x, "col", [(i, i ^ k) for i in range(16)])


def z_send(x, s):
    return lax.ppermute(x, "row", [(i, (i + 2 * s) % 16) for i in range(16)])


COL_ORDER = (2, 6, 1, 4, 3, 7, 5)


def on_chip_row(source_of, keep=lambda y, core: True):
    pairs = []
    for row in range(16):
        for col in range(16):
            y, core = row % 2, col % 2
            if keep(y, core):
                from_y, from_core = source_of(y, core)
                pairs.append(((row - y + from_y) * 16 + col - core + from_core, row * 16 + col))
    return pairs


def on_device(hidden, weight, out_grad):
    shape = jax.ShapeDtypeStruct
    hidden_near, weight_near = call(
        load_kernel,
        [shape(hidden.shape, BF), shape(weight.shape, BF)],
        [pltpu.SemaphoreType.DMA((2,))],
        hidden,
        weight,
        place=far,
    )
    tokens, units = hidden.shape
    width = weight.shape[1]
    both = ("row", "col")
    _, y, _, core = position()
    same = y == core
    opposite = on_chip_row(lambda y, core: (1 - y, 1 - core), lambda y, core: y != core)

    beside = on_chip_row(lambda y, core: (y, 1 - core) if y == core else (1 - y, core))
    first = lax.ppermute(out_grad, both, beside)
    second = lax.ppermute(out_grad, both, opposite)
    ring = [None] * 8
    ring[0] = jnp.stack([jnp.where(same, out_grad, first), jnp.where(same, first, second)])
    for s in range(1, 4):
        ring[s] = z_send(ring[s - 1], -1)
        ring[8 - s] = z_send(ring[(9 - s) % 8], 1)
    ring[4] = z_send(ring[3], -1)
    other_weight = col_send(weight, 1)

    blocks = [None] * 8
    blocks[0] = hidden
    blocks[1] = col_send(hidden, 2)
    for k in (2, 6, 4):
        blocks[k] = col_send(hidden, 2 * k)
        blocks[k + 1] = col_send(blocks[1], 2 * k)

    half = 8 * tokens
    grad_out = call(
        grad_kernel,
        [shape((tokens, units), F32)]
        + [shape((tokens, units + 128), BF)] * 7
        + [shape((half, width), BF)] * 2,
        [
            pltpu.VMEM((8, 2, tokens, width), BF),
            pltpu.VMEM((half, 2 * width), BF),
            pltpu.VMEM((half, units), F32),
        ],
        *ring,
        weight_near,
        other_weight,
    )
    proj_out = call(
        proj_kernel,
        [shape((tokens, 2 * width), F32)]
        + [shape((tokens, 2 * width + 128), BF)] * 7
        + [shape((half, units), BF)],
        [
            pltpu.VMEM((half, units), BF),
            pltpu.VMEM((8, tokens, 2 * width), F32),
        ],
        hidden_near,
        *blocks[1:],
        weight_near,
        other_weight,
    )
    got_grad = [col_send(grad_out[k], 2 * k) for k in COL_ORDER]
    got_proj = [z_send(proj_out[s], s) for s in (4, 3, 5, 2, 6, 1, 7)]
    g_own, g_swap = grad_out[8], col_send(grad_out[9], 1)
    h_own, h_swap = proj_out[8], col_send(proj_out[8], 1)

    dims = (((0,), (0,)), ((), ()))
    weight_grad = lax.dot_general(h_own, g_own, dims, preferred_element_type=F32)
    weight_grad += lax.dot_general(h_swap, g_swap, dims, preferred_element_type=F32)
    weight_grad = weight_grad / jnp.sqrt(F32(16 * tokens))

    (early,) = call(
        sum_hidden_kernel, [shape((tokens, units), F32)], [], grad_out[0], *got_grad[:5]
    )
    (hidden_grad,) = call(sum_hidden_kernel, [shape((tokens, units), BF)], [], early, *got_grad[5:])
    sum_own, sum_other, sum_first = call(
        sum_proj_kernel, [shape((tokens, width), F32)] * 3, [], proj_out[0], *got_proj
    )
    beside = on_chip_row(lambda y, core: (1 - y, core) if y == core else (y, 1 - core))
    first = lax.ppermute(sum_first, both, beside)
    second = lax.ppermute(sum_other, both, opposite)
    projected = (first + jnp.where(same, sum_own, second)).astype(BF)
    return (projected, hidden_grad, weight_grad)


def solution(mesh):
    return jax.shard_map(
        on_device,
        mesh=mesh,
        in_specs=(P("col", "row"), P("row", "col"), P("row", "col")),
        out_specs=(P("row", "col"), P("col", "row"), P("row", "col")),
        check_vma=False,
    )
```
